128 devices in a mesh: grp: 4 (over y_lo, core), mem: 32 (over x, y_hi, z).
Axes of the slice: x: 4, y: 4 (y_hi: 2, y_lo: 2; y = y_hi * 2 + y_lo), z: 4, core: 2. Of those that a mesh axis runs over, the one named last changes fastest.
Arguments:
- amplitudes: float32 [192, 4, 32, 2000], P('mem', 'grp'), may hold values from -6 to 6
- singles: float32 [250, 2000], replicated, may hold values from -5 to 5
- pair_list: int32 [192, 2], replicated, may hold values from 0 to 249, as said below
- mirror: int32 [192], replicated, may hold values from 0 to 191, as said below
- slab_rows: int32 [2048, 2], P('grp'), may hold values from 0 to 1999
- occ_energy: float32 [250], replicated, may hold values from -1 to -0.2
- vir_energy: float32 [2000], replicated, may hold values from 0.2 to 1
- integrals: float32 [2048, 4, 32, 2000], P('grp', None, 'mem'), may hold values from -0.01171875 to 0.01171875
Outputs:
- update: float32 [192, 2048], P('mem', 'grp')
The draws below stay inside these ranges and needn't reach their ends.
Inputs may be any that keep to these rules, and one draw needn't show every extreme that they name: `pair_list`: each row holds two occupied orbitals i < j; no pair appears twice. mirror[mirror[p]] = p and mirror[p] != p; a pair p of owner block k = p // 6 is mapped into owner block (k + 32 / 2) mod 32.
All inputs are finite; a program needn't handle non-finite values.
Results may differ from the reference program's by a relative error of at most 0.000073.
Values sent between devices are 32-bit elements; how exact they have to be, the bound alone decides.
No kernel may reach another device: no remote copies, remote signals or barrier semaphores. Data moves between devices by JAX's collectives and lax.ppermute only.
A program may use at most 128 MiB of HBM per device.

```python
import jax
import jax.numpy as jnp
from jax import lax

NO = 250
NV = 2000
AB = 2048
PAIR_DEV = 6
CBQ = 32
PAIRS = 192
N_GRP = 4
N_MEM = 32


def draw_pair_list(key, part):
    pair_codes = jax.random.permutation(key, NO * NO)
    first_orb = pair_codes // NO
    second_orb = pair_codes % NO
    ranking = jnp.argsort((first_orb >= second_orb).astype(jnp.int32), stable=True)
    chosen = pair_codes[ranking[:PAIRS]]
    return jnp.stack([chosen // NO, chosen % NO], axis=1).astype(jnp.int32)


def draw_mirror(key, part):
    half_owners = N_MEM // 2
    owner_keys = jax.random.split(jax.random.fold_in(key, 17), half_owners)
    slot_perms = jax.vmap(lambda one_key: jax.random.permutation(one_key, PAIR_DEV))(owner_keys)
    inverse = jnp.argsort(slot_perms, axis=1)
    owner_ids = jnp.arange(half_owners, dtype=jnp.int32)[:, None]
    lower = (owner_ids + half_owners) * PAIR_DEV + slot_perms
    upper = owner_ids * PAIR_DEV + inverse
    return jnp.concatenate([lower.reshape(-1), upper.reshape(-1)]).astype(jnp.int32)


def place_ends(entries, key, smallest, largest):
    extent = entries.shape
    index_at = [jax.random.randint(jax.random.fold_in(key, axis), (), 0, extent[axis]) for axis in range(len(extent))]
    entries = entries.at[tuple(index_at)].set(smallest)
    longest = extent.index(max(extent))
    index_at[longest] = (index_at[longest] + 1) % extent[longest]
    return entries.at[tuple(index_at)].set(largest)


def steps_of(own_key, shape, cuts, least, high):
    factor_of = 1.0
    for dim, blocks in cuts:
        draws = jax.random.uniform(jax.random.fold_in(jax.random.fold_in(own_key, 6), dim), (blocks,), jnp.float32, least / len(cuts), high / len(cuts))
        factor_of = factor_of * jnp.repeat(jnp.exp(draws), shape[dim] // blocks).reshape((-1,) + (1,) * (len(shape) - 1 - dim))
    return factor_of


def noise(rng, dims, width, most, pieces=(), held_as=jnp.bfloat16):
    result = jax.random.normal(rng, dims, jnp.float32) * width
    if len(pieces) > 0:
        result = steps_of(rng, dims, pieces, -0.22, 0.18) * result
    return jnp.clip(result, min=-most, max=most).astype(held_as)


def setup_inputs(seed: int = 0) -> dict:
    splits = jax.random.split(jax.random.key(seed), 9)
    amplitudes = noise(splits[0], (PAIRS, N_GRP, CBQ, NV), 1.0, 6.0, ((0, 32), (1, 4)), jnp.float32)
    singles = noise(splits[1], (NO, NV), 0.8, 5.0, (), jnp.float32)
    pair_list = draw_pair_list(jax.random.fold_in(splits[8], 71), 0)
    mirror = draw_mirror(jax.random.fold_in(splits[8], 71), 0)
    slab_rows = place_ends(jax.random.randint(splits[4], (AB, 2), 0, NV), jax.random.fold_in(splits[4], 1), 0, NV - 1).astype(jnp.int32)
    occ_energy = jnp.clip(jax.random.uniform(splits[5], (NO,), jnp.float32, -1.0, -0.2), -1.0, -0.2)
    vir_energy = jnp.clip(jax.random.uniform(splits[6], (NV,), jnp.float32, 0.2, 1.0), 0.2, 1.0)
    integrals = noise(splits[7], (AB, N_GRP, CBQ, NV), (N_GRP * CBQ * NV) ** -0.5, 0.01171875, ((0, 4), (2, 32)), jnp.float32)
    return dict(amplitudes=amplitudes, singles=singles, pair_list=pair_list, mirror=mirror, slab_rows=slab_rows, occ_energy=occ_energy, vir_energy=vir_energy, integrals=integrals)


def reference(amplitudes, singles, pair_list, mirror, slab_rows, occ_energy, vir_energy, integrals):
    pair_total = amplitudes.shape[0]
    window_c = N_GRP * CBQ
    blocks = amplitudes.reshape(pair_total, window_c, NV)
    unpacked = blocks - jnp.take(blocks, mirror, axis=0)
    first_rows = jnp.take(singles, pair_list[:, 0], axis=0)
    second_rows = jnp.take(singles, pair_list[:, 1], axis=0)
    tau_full = unpacked + first_rows[:, :window_c, None] * second_rows[:, None, :] - second_rows[:, :window_c, None] * first_rows[:, None, :]
    flat_ints = integrals.reshape(integrals.shape[0], -1)
    ladder = 0.5 * lax.dot_general(tau_full.reshape(pair_total, -1), flat_ints, (((1,), (1,)), ((), ())), precision=lax.Precision.HIGHEST, preferred_element_type=jnp.float32)
    vir_first = jnp.take(vir_energy, slab_rows[:, 0])
    vir_second = jnp.take(vir_energy, slab_rows[:, 1])
    occ_first = jnp.take(occ_energy, pair_list[:, 0])
    occ_second = jnp.take(occ_energy, pair_list[:, 1])
    denominator = vir_first[None, :] + vir_second[None, :] - occ_first[:, None] - occ_second[:, None]
    return ladder / denominator
```

```python
import functools

import jax
import jax.numpy as jnp
from jax import lax
from jax.experimental import pallas as pl
from jax.experimental.pallas import tpu as pltpu
from jax.sharding import PartitionSpec as P

LANES = 128
BF16 = jnp.bfloat16
F32 = jnp.float32


def split(value):
    high = value.astype(BF16)
    return high, (value - high.astype(F32)).astype(BF16)


def pack_kernel(stored_ref, packed_ref, *, chunks):
    offsets, width = stored_ref.shape[2:]
    flat = packed_ref.reshape(offsets * chunks, LANES)
    for first in range(0, offsets, 8):
        for k in range(chunks):
            size = min(LANES, width - k * LANES)
            tile = stored_ref[0, 0, first : first + 8, k * LANES : k * LANES + size]
            if size < LANES:
                tile = jnp.concatenate([tile, jnp.zeros((8, LANES - size), F32)], axis=1)
            flat[pl.ds(first * chunks + k, 8, stride=chunks), :] = tile


def pack(stored, chunks):
    pairs, _, offsets, width = stored.shape
    return pl.pallas_call(
        functools.partial(pack_kernel, chunks=chunks),
        grid=(pairs,),
        in_specs=[pl.BlockSpec((1, 1, offsets, width), lambda p: (p, 0, 0, 0))],
        out_specs=pl.BlockSpec((offsets, chunks, LANES), lambda p: (0, p, 0)),
        out_shape=jax.ShapeDtypeStruct((offsets, pairs * chunks, LANES), F32),
        name="pack",
    )(stored)


def unpack_kernel(mirror_ref, blocks_ref, out_ref):
    def step(p, _):
        out_ref[p] = blocks_ref[p] - blocks_ref[mirror_ref[p]]
        return 0

    lax.fori_loop(0, out_ref.shape[0], step, 0, unroll=8)


def unpack(mirror, blocks):
    pairs, chunks, lanes = blocks.shape
    return pl.pallas_call(
        unpack_kernel,
        in_specs=[pl.BlockSpec(memory_space=pltpu.SMEM), pl.BlockSpec(memory_space=pltpu.VMEM)],
        out_specs=pl.BlockSpec(memory_space=pltpu.VMEM),
        out_shape=jax.ShapeDtypeStruct((pairs // 2, chunks, lanes), F32),
        name="unpack",
    )(mirror, blocks)


def early_kernel(member_ref, first_ref, second_ref, ints_ref, singles_ref, high_ref, low_ref, lhs):
    q = pl.program_id(0)
    pairs, width = first_ref.shape
    padded = lhs.shape[1]

    @pl.when(q == 0)
    def _():
        lhs[:, width // LANES * LANES :] = jnp.zeros((2 * pairs, padded - width // LANES * LANES), BF16)

    high, low = split(ints_ref[0])
    high_ref[0, :width] = high
    low_ref[0, :width] = low
    tail = jnp.zeros((padded - width, high.shape[1]), BF16)
    high_ref[0, width:] = tail
    low_ref[0, width:] = tail

    lane = lax.broadcasted_iota(jnp.int32, (pairs, LANES), 1)
    chosen = lane == q * 32 + member_ref[0]
    first_c = jnp.sum(jnp.where(chosen, first_ref[:, :LANES], 0.0), axis=1, keepdims=True)
    second_c = jnp.sum(jnp.where(chosen, second_ref[:, :LANES], 0.0), axis=1, keepdims=True)
    for start in range(0, width, LANES):
        size = min(LANES, width - start)
        at = slice(start, start + size)
        part = first_c * second_ref[:, at] - second_c * first_ref[:, at]
        part_high, part_low = split(part)
        lhs[:pairs, at] = part_high
        lhs[pairs:, at] = part_low
    both = jnp.dot(lhs[...], high_ref[0], preferred_element_type=F32)
    total = both[:pairs] + both[pairs:]
    total += jnp.dot(lhs[:pairs], low_ref[0], preferred_element_type=F32)

    @pl.when(q == 0)
    def _():
        singles_ref[...] = total

    @pl.when(q > 0)
    def _():
        singles_ref[...] += total


def early(member, first, second, ints, padded):
    pairs, width = first.shape
    quarters, _, rows = ints.shape
    whole = lambda q: (0, 0)
    return pl.pallas_call(
        early_kernel,
        grid=(quarters,),
        in_specs=[
            pl.BlockSpec(memory_space=pltpu.SMEM),
            pl.BlockSpec((pairs, width), whole),
            pl.BlockSpec((pairs, width), whole),
            pl.BlockSpec((1, width, rows), lambda q: (q, 0, 0)),
        ],
        out_specs=[
            pl.BlockSpec((pairs, rows), whole),
            pl.BlockSpec((1, padded, rows), lambda q: (q, 0, 0)),
            pl.BlockSpec((1, padded, rows), lambda q: (q, 0, 0)),
        ],
        out_shape=[
            jax.ShapeDtypeStruct((pairs, rows), F32),
            jax.ShapeDtypeStruct((quarters, padded, rows), BF16),
            jax.ShapeDtypeStruct((quarters, padded, rows), BF16),
        ],
        scratch_shapes=[pltpu.VMEM((2 * pairs, padded), BF16)],
        name="early",
    )(member, first, second, ints)


def fill(lhs, values_ref):
    pairs, chunks, _ = values_ref.shape
    flat = values_ref.reshape(pairs * chunks, LANES)
    for first in range(0, pairs, 16):
        for k in range(chunks):
            tile = flat[pl.ds(first * chunks + k, 16, stride=chunks), :]
            high, low = split(tile)
            at = slice(k * LANES, (k + 1) * LANES)
            lhs[first : first + 16, at] = high
            lhs[pairs + first : pairs + first + 16, at] = low


def product(lhs, high, low):
    pairs = lhs.shape[0] // 2
    both = jnp.dot(lhs[...], high, preferred_element_type=F32)
    return both[:pairs] + both[pairs:] + jnp.dot(lhs[:pairs], low, preferred_element_type=F32)


def contract_kernel(order_ref, *refs, count, has_sum, last):
    values, rest = refs[:count], refs[count:]
    high_ref, low_ref, *rest = rest
    pairs = values[0].shape[0]
    step = pl.program_id(0)
    if has_sum:
        sum_ref, *rest = rest
    if last:
        singles_ref, *rest = rest
    out_ref, lhs, total_ref = rest

    for n in range(count):

        @pl.when(step == n)
        def _(n=n):
            fill(lhs, values[n])

    part = product(lhs, high_ref[0], low_ref[0])
    start = sum_ref[...] if has_sum else jnp.zeros_like(part)
    total = jnp.where(step == 0, start, total_ref[...]) + part if count > 1 else start + part
    if count > 1:
        total_ref[...] = total

    @pl.when(step == count - 1)
    def _():
        if not last:
            out_ref[...] = total
        else:
            rows = total.shape[1]
            per = rows // LANES
            for side in range(2):
                mine = singles_ref[side * pairs : (side + 1) * pairs]
                full = 0.5 * (mine + total if side == 0 else mine - total)
                for first in range(0, pairs, 8):
                    for n in range(per):
                        at = pl.ds((side * pairs + first) * per + n, 8, stride=per)
                        out_ref[at, :] = full[first : first + 8, n * LANES : (n + 1) * LANES]


def contract(order, values, high, low, total=None, singles=None):
    count = len(values)
    pairs, chunks, _ = values[0].shape
    _, padded, rows = high.shape
    vmem = lambda a: pl.BlockSpec(a.shape, lambda n, order: (0,) * a.ndim)
    extra = [a for a in (total, singles) if a is not None]
    part = pl.BlockSpec((1, padded, rows), lambda n, order: (order[n], 0, 0))
    out = (pairs, rows) if singles is None else (2 * pairs * rows // LANES, LANES)
    return pl.pallas_call(
        functools.partial(contract_kernel, count=count, has_sum=total is not None, last=singles is not None),
        grid_spec=pltpu.PrefetchScalarGridSpec(
            num_scalar_prefetch=1,
            grid=(count,),
            in_specs=[vmem(v) for v in values] + [part, part] + [vmem(a) for a in extra],
            out_specs=pl.BlockSpec(out, lambda n, order: (0, 0)),
            scratch_shapes=[pltpu.VMEM((2 * pairs, padded), BF16), pltpu.VMEM((pairs, rows), F32)],
        ),
        out_shape=jax.ShapeDtypeStruct(out, F32),
        name=f"contract_{count}_{len(extra)}",
    )(order, *values, high, low, *extra)


def finish_kernel(slot_ref, first_ref, second_ref, virtual_ref, parts_ref, out_ref, sums):
    pairs, rows = out_ref.shape
    per = rows // LANES
    total = parts_ref[0]
    for n in range(1, parts_ref.shape[0]):
        total += parts_ref[n]
    for a in range(pairs):
        sums[a] = total[a * per : (a + 1) * per]
    virtual = virtual_ref[...]
    for a in range(pairs):
        denominator = virtual - first_ref[a] - second_ref[a]
        value = sums[slot_ref[a]] / denominator
        for n in range(per):
            out_ref[a : a + 1, n * LANES : (n + 1) * LANES] = value[n : n + 1]


def finish(slot, first, second, virtual, parts):
    pairs = slot.shape[0]
    per = virtual.shape[0]
    smem = pl.BlockSpec(memory_space=pltpu.SMEM)
    vmem = pl.BlockSpec(memory_space=pltpu.VMEM)
    return pl.pallas_call(
        finish_kernel,
        in_specs=[smem, smem, smem, vmem, vmem],
        out_specs=vmem,
        out_shape=jax.ShapeDtypeStruct((pairs, per * LANES), F32),
        scratch_shapes=[pltpu.VMEM((pairs, per, LANES), F32)],
        name="finish",
    )(slot, first, second, virtual, parts)


def take(table, index):
    return table.at[index].get(mode="promise_in_bounds")


def body(amplitudes, singles, pair_list, mirror, slab_rows, occ_energy, vir_energy, integrals):
    owners = lax.axis_size("mem")
    groups = lax.axis_size("grp")
    member = lax.axis_index("mem")
    group = lax.axis_index("grp")
    pair_dev, _, _, width = amplitudes.shape
    pair_total = pair_dev * owners
    half = pair_total // 2
    rows = integrals.shape[0]
    chunks = -(-width // LANES)
    padded = chunks * LANES

    packed = pack(amplitudes, chunks)
    blocks = lax.all_to_all(packed, "mem", 0, 0).reshape(pair_total, chunks, LANES)

    ordered = jnp.concatenate([pair_list[:half], take(pair_list, mirror[:half])], axis=0)
    first = take(singles, ordered[:, 0])
    second = take(singles, ordered[:, 1])
    ints = jnp.transpose(integrals[:, :, 0, :], (1, 2, 0))
    from_singles, high, low = early(member.reshape(1), first, second, ints, padded)

    own_pairs = lax.dynamic_slice_in_dim(pair_list, member * pair_dev, pair_dev, 0)
    own_mirror = lax.dynamic_slice_in_dim(mirror, member * pair_dev, pair_dev, 0)
    slot = jnp.where(member < owners // 2, jnp.arange(pair_dev, dtype=jnp.int32), own_mirror % pair_dev)
    virtual = take(vir_energy, slab_rows[:, 0]) + take(vir_energy, slab_rows[:, 1])
    virtual = virtual.reshape(rows // LANES, LANES)
    first_occ, second_occ = take(occ_energy, own_pairs[:, 0]), take(occ_energy, own_pairs[:, 1])
    blocks, from_singles, high, low, slot, virtual, first_occ, second_occ = lax.optimization_barrier(
        (blocks, from_singles, high, low, slot, virtual, first_occ, second_occ)
    )

    unpacked = unpack(mirror, blocks)
    swap = lambda v, k: lax.ppermute(v, "grp", [(i, i ^ k) for i in range(groups)])
    other_chip = swap(unpacked, 2)
    other_core = swap(unpacked, 1)
    across = swap(other_chip, 1)
    total = contract(jnp.stack([group, group ^ 1]), [unpacked, other_core], high, low)
    total = contract((group ^ 2).reshape(1), [other_chip], high, low, total)
    parts = contract((group ^ 3).reshape(1), [across], high, low, total, from_singles)
    parts = lax.all_to_all(parts.reshape(owners, -1, LANES), "mem", 0, 0)
    return finish(slot, first_occ, second_occ, virtual, parts)


def solution(mesh):
    in_specs = (
        P("mem", "grp", None, None),
        P(),
        P(),
        P(),
        P("grp", None),
        P(),
        P(),
        P("grp", None, "mem", None),
    )
    out_specs = P("mem", "grp")
    return jax.shard_map(body, mesh=mesh, in_specs=in_specs, out_specs=out_specs, check_vma=False)
```

```python
import functools

import jax
import jax.numpy as jnp
from jax import lax
from jax.experimental import pallas as pl
from jax.experimental.pallas import tpu as pltpu
from jax.sharding import PartitionSpec as P

LANES = 128
BF16 = jnp.bfloat16
F32 = jnp.float32
X, Y_HI, Z = 4, 2, 4
CORES = 2

VMEM_SPEC = pl.BlockSpec(memory_space=pltpu.VMEM)
SMEM_SPEC = pl.BlockSpec(memory_space=pltpu.SMEM)
HBM_SPEC = pl.BlockSpec(memory_space=pltpu.HBM)


def vmem(array):
    return pltpu.with_memory_space_constraint(array, pltpu.VMEM)


def hbm(array):
    return pltpu.with_memory_space_constraint(array, pltpu.HBM)


def params(mebibytes):
    return pltpu.CompilerParams(vmem_limit_bytes=mebibytes << 20)


def split(value):
    high = value.astype(BF16)
    return high, (value - high.astype(F32)).astype(BF16)


def product(lhs, high, low):
    pairs = lhs.shape[0] // 2
    both = jnp.dot(lhs[...], high, preferred_element_type=F32)
    return both[:pairs] + both[pairs:] + jnp.dot(lhs[:pairs], low, preferred_element_type=F32)


def split_rows(values, high_ref, low_ref):
    width, rows = values.shape
    high, low = split(values)
    high_ref[:width] = high
    low_ref[:width] = low
    tail = jnp.zeros((high_ref.shape[0] - width, rows), BF16)
    high_ref[width:] = tail
    low_ref[width:] = tail


def pack_kernel(stored_ref, packed_ref, *, chunks):
    pair = pl.program_id(0)
    width = stored_ref.shape[3]
    for x in range(X):
        tile = stored_ref[0, 0, x * Y_HI * Z : (x + 1) * Y_HI * Z, :]
        tile = jnp.concatenate([tile, jnp.zeros((Y_HI * Z, chunks * LANES - width), F32)], axis=1)
        tile = tile.reshape(Y_HI * Z, chunks, LANES)
        at = pl.ds(pl.multiple_of(pair * chunks, chunks), chunks)
        for y in range(Y_HI):
            packed_ref[x * Z : (x + 1) * Z, y, at, :] = tile[y * Z : (y + 1) * Z]


def pack(stored, chunks):
    pairs, _, offsets, width = stored.shape
    return pl.pallas_call(
        functools.partial(pack_kernel, chunks=chunks),
        grid=(pairs,),
        in_specs=[pl.BlockSpec((1, 1, offsets, width), lambda p: (p, 0, 0, 0))],
        out_specs=VMEM_SPEC,
        out_shape=pltpu.VMEM((X * Z, Y_HI, pairs * chunks, LANES), F32),
        compiler_params=params(8),
        name="pack",
    )(stored)


def unpack_kernel(place_ref, mirror_ref, lower_ref, upper_ref, out_ref, *, sources):
    step = pl.program_id(0)
    pairs = lower_ref.shape[2]
    for n in range(sources):
        source = step * sources + n
        owner = source // Z * (Y_HI * Z) + place_ref[0] * Z + source % Z
        for a in range(pairs):
            slot = lax.rem(mirror_ref[owner * pairs + a], pairs)
            out_ref[:, source * pairs + a, :] = lower_ref[n, 0, a] - upper_ref[n, 0, slot]


def unpack(place, mirror, blocks):
    count, _, pairs, chunks, lanes = blocks.shape
    half, steps = count // 2, 2
    side = lambda shift: pl.BlockSpec(
        (half // steps, 1, pairs, chunks, lanes), lambda n, place, mirror: (n + shift, place[1], 0, 0, 0)
    )
    return pl.pallas_call(
        functools.partial(unpack_kernel, sources=half // steps),
        grid_spec=pltpu.PrefetchScalarGridSpec(
            num_scalar_prefetch=2,
            grid=(steps,),
            in_specs=[side(0), side(steps)],
            out_specs=VMEM_SPEC,
        ),
        out_shape=pltpu.VMEM((chunks, half * pairs, lanes), F32),
        compiler_params=params(8),
    )(place, mirror, blocks, blocks)


def exact(chosen, table, contract):
    total = None
    for _ in range(3):
        piece = table.astype(BF16)
        table = table - piece.astype(F32)
        part = lax.dot_general(chosen, piece, (contract, ((), ())), preferred_element_type=F32)
        total = part if total is None else total + part
    return total


def quarter(q, rows, member, lhs, ints, high_ref, low_ref, copy):
    _, pairs, width = rows.shape
    chosen = lax.broadcasted_iota(jnp.int32, (pairs, LANES), 1) == q * (X * Y_HI * Z) + member
    first_c = jnp.sum(jnp.where(chosen, rows[0, :, :LANES], 0.0), axis=1, keepdims=True)
    second_c = jnp.sum(jnp.where(chosen, rows[1, :, :LANES], 0.0), axis=1, keepdims=True)
    for start in range(0, width, LANES):
        at = slice(start, min(start + LANES, width))
        part = first_c * rows[1, :, at] - second_c * rows[0, :, at]
        part_high, part_low = split(part)
        lhs[:pairs, at] = part_high
        lhs[pairs:, at] = part_low
    copy.wait()
    split_rows(ints[...], high_ref, low_ref)
    return product(lhs, high_ref[...], low_ref[...])


def clear(lhs, width):
    full = width // LANES * LANES
    lhs[:, full:] = jnp.zeros((lhs.shape[0], lhs.shape[1] - full), BF16)


def early_kernel(
    member_ref, pairs_ref, singles_ref, ints_ref, sum_ref, high_out, low_out,
    ints, sems, rows, lhs, high, low, out_sems,
):
    count, width, _ = ints.shape
    copies = [pltpu.make_async_copy(ints_ref.at[q], ints.at[q], sems.at[q]) for q in range(count)]
    for copy in copies:
        copy.start()
    pairs, orbitals = pairs_ref.shape[0], singles_ref.shape[1]
    clear(lhs, width)
    orbital = lax.broadcasted_iota(jnp.int32, (pairs, orbitals), 1)
    for side in range(2):
        chosen = (orbital == pairs_ref[:, side : side + 1]).astype(F32).astype(BF16)
        rows[side] = exact(chosen, singles_ref[...], ((1,), (1,)))
    total = None
    outs = []
    for q in range(count):
        slot = q % 2
        for out in outs[2 * (q - 2) : 2 * (q - 1)] if q > 1 else []:
            out.wait()
        part = quarter(q, rows, member_ref[0], lhs, ints.at[q], high.at[slot], low.at[slot], copies[q])
        total = part if total is None else total + part
        for n, (here, there) in enumerate(((high, high_out), (low, low_out))):
            outs.append(pltpu.make_async_copy(here.at[slot], there.at[q], out_sems.at[n, q]))
            outs[-1].start()
    sum_ref[...] = total
    for out in outs[-4:]:
        out.wait()


def early(member, pairs, singles, ints, padded):
    count = pairs.shape[0]
    quarters, width, rows = ints.shape
    return pl.pallas_call(
        early_kernel,
        in_specs=[SMEM_SPEC] + [VMEM_SPEC] * 2 + [HBM_SPEC],
        out_specs=[VMEM_SPEC] + [HBM_SPEC] * 2,
        out_shape=[jax.ShapeDtypeStruct((count, rows), F32)] + [pltpu.HBM((quarters, padded, rows), BF16)] * 2,
        scratch_shapes=[
            pltpu.VMEM((quarters, width, rows), F32),
            pltpu.SemaphoreType.DMA((quarters,)),
            pltpu.VMEM((2, count, width), F32),
            pltpu.VMEM((2 * count, padded), BF16),
            pltpu.VMEM((2, padded, rows), BF16),
            pltpu.VMEM((2, padded, rows), BF16),
            pltpu.SemaphoreType.DMA((2, quarters)),
        ],
        compiler_params=params(48),
        name="early",
    )(member, pairs, singles, ints)


def virtual_kernel(slab_ref, energies_ref, out_ref):
    rows = slab_ref.shape[1]
    coarse = lax.broadcasted_iota(jnp.int32, (energies_ref.shape[1], rows), 0)
    fine = lax.broadcasted_iota(jnp.int32, (LANES, rows), 0)
    total = None
    for side in range(2):
        orbital = slab_ref[side : side + 1, :]
        chosen = (coarse == orbital // LANES).astype(F32).astype(BF16)
        rest, columns = energies_ref[...], None
        for _ in range(3):
            piece = rest.astype(BF16)
            rest = rest - piece.astype(F32)
            part = jnp.dot(piece, chosen, preferred_element_type=F32)
            columns = part if columns is None else columns + part
        energy = jnp.sum(jnp.where(fine == orbital % LANES, columns, 0.0), axis=0, keepdims=True)
        total = energy if total is None else total + energy
    for n in range(rows // LANES):
        out_ref[n : n + 1, :] = total[:, n * LANES : (n + 1) * LANES]


def virtual_sums(slab, energies):
    return pl.pallas_call(
        virtual_kernel,
        in_specs=[VMEM_SPEC] * 2,
        out_specs=VMEM_SPEC,
        out_shape=jax.ShapeDtypeStruct((slab.shape[1] // LANES, LANES), F32),
        compiler_params=params(8),
        name="virtual",
    )(slab, energies)


def fill(lhs, values):
    half = lhs.shape[0] // 2
    row = 0
    for value_ref in values:
        chunks, pairs, _ = value_ref.shape
        for k in range(chunks):
            high, low = split(value_ref[k])
            at = slice(k * LANES, (k + 1) * LANES)
            lhs[row : row + pairs, at] = high
            lhs[half + row : half + row + pairs, at] = low
        row += pairs


def own_kernel(place_ref, value_ref, high_in, low_in, high_ref, low_ref, out_ref, sems, lhs):
    quarters = high_ref.shape[0]
    order = [place_ref[2] ^ n for n in range(quarters)]
    copies = [
        pltpu.make_async_copy(there.at[q], here.at[q], sems.at[n, m])
        for m, q in enumerate(order)
        for n, (there, here) in enumerate(((high_in, high_ref), (low_in, low_ref)))
    ]
    for copy in copies:
        copy.start()
    fill(lhs, [value_ref])
    copies[0].wait()
    copies[1].wait()
    pairs = value_ref.shape[1]
    out_ref[:pairs] = product(lhs, high_ref[order[0]], low_ref[order[0]])
    out_ref[pairs:] = jnp.zeros_like(out_ref[pairs:])
    for copy in copies[2:]:
        copy.wait()


def own(place, value, high, low):
    _, pairs, _ = value.shape
    quarters, padded, rows = high.shape
    return pl.pallas_call(
        own_kernel,
        in_specs=[SMEM_SPEC, VMEM_SPEC, HBM_SPEC, HBM_SPEC],
        out_specs=[VMEM_SPEC] * 3,
        out_shape=[
            pltpu.VMEM(high.shape, BF16),
            pltpu.VMEM(low.shape, BF16),
            pltpu.VMEM((2 * pairs, rows), F32),
        ],
        scratch_shapes=[pltpu.SemaphoreType.DMA((2, quarters)), pltpu.VMEM((2 * pairs, padded), BF16)],
        compiler_params=params(8),
        name="own",
    )(place, vmem(value), hbm(high), hbm(low))


def contract_kernel(place_ref, *refs, flip, first, count, fresh, last):
    values, (high_ref, low_ref, *rest) = refs[:count], refs[count:]
    if not fresh:
        sum_ref, *rest = rest
    if last:
        singles_ref, *rest = rest
    out_ref, lhs = rest
    pairs = lhs.shape[0] // 2
    fill(lhs, values)
    quarter = place_ref[2] ^ flip
    part = product(lhs, high_ref[quarter], low_ref[quarter])
    if not last:
        for row in range(0, out_ref.shape[0], pairs):
            at = slice(row, row + pairs)
            if fresh:
                out_ref[at] = part if row == first else jnp.zeros_like(part)
            else:
                out_ref[at] = sum_ref[at] + part if row == first else sum_ref[at]
        return
    total = [sum_ref[row : row + pairs] + (part if row == first else 0.0) for row in (0, pairs)]
    per = part.shape[1] // LANES
    group = pairs // 2
    sides = singles_ref.shape[0] // 2
    for y, sums in enumerate(total):
        place = place_ref[y]
        for x in range(2):
            for mirrored in range(2):
                row = mirrored * sides + x * Y_HI * group + place * group
                mine = singles_ref[pl.ds(pl.multiple_of(row, 8), group), :]
                ours = sums[x * group : (x + 1) * group]
                full = 0.5 * (mine - ours if mirrored else mine + ours)
                for a in range(0, group, 8):
                    for n in range(per):
                        at = pl.ds((row + a) * per + n, 8, stride=per)
                        out_ref[at, :] = full[a : a + 8, n * LANES : (n + 1) * LANES]


def contract(place, flip, values, first, high, low, total=None, singles=None):
    count = len(values)
    _, pairs, _ = values[0].shape
    _, padded, rows = high.shape
    last = singles is not None
    inputs = [*values, high, low] + [a for a in (total, singles) if a is not None]
    out = (4 * pairs * rows // LANES, LANES) if last else (2 * pairs, rows)
    return pl.pallas_call(
        functools.partial(
            contract_kernel, flip=flip, first=first, count=count, fresh=total is None, last=last
        ),
        in_specs=[SMEM_SPEC] + [VMEM_SPEC] * len(inputs),
        out_specs=VMEM_SPEC,
        out_shape=pltpu.VMEM(out, F32),
        scratch_shapes=[pltpu.VMEM((2 * pairs * count, padded), BF16)],
        compiler_params=params(8),
    )(place, *(vmem(a) for a in inputs))


def finish_kernel(member_ref, mirror_ref, pairs_ref, occupied_ref, virtual_ref, parts_ref, out_ref, sums):
    pairs, rows = out_ref.shape
    per = rows // LANES
    member = member_ref[0]
    total = parts_ref[0]
    for n in range(1, parts_ref.shape[0]):
        total += parts_ref[n]
    for a in range(pairs):
        sums[a] = total[a * per : (a + 1) * per]
    for a in range(pairs):
        pair = member * pairs + a
        denominator = virtual_ref[...] - occupied_ref[pairs_ref[0, pair]] - occupied_ref[pairs_ref[1, pair]]
        slot = jnp.where(member < parts_ref.shape[0] // 2, a, lax.rem(mirror_ref[pair], pairs))
        value = sums[slot] / denominator
        for n in range(per):
            out_ref[a : a + 1, n * LANES : (n + 1) * LANES] = value[n : n + 1]


def finish(member, mirror, pairs, occupied, virtual, parts):
    _, block, _ = parts.shape
    per = virtual.shape[0]
    count = block // per
    return pl.pallas_call(
        finish_kernel,
        in_specs=[SMEM_SPEC] * 4 + [VMEM_SPEC] * 2,
        out_specs=VMEM_SPEC,
        out_shape=jax.ShapeDtypeStruct((count, per * LANES), F32),
        scratch_shapes=[pltpu.VMEM((count, per, LANES), F32)],
        compiler_params=params(8),
        name="finish",
    )(member, mirror, pairs, occupied, virtual, parts)


def neighbour(device):
    group, member = divmod(device, X * Y_HI * Z)
    y_lo, core = divmod(group, CORES)
    x, place = divmod(member, Y_HI * Z)
    y_hi, z = divmod(place, Z)
    y = y_hi * 2 + y_lo
    y = y + 1 if y % 2 else y - 1
    y_hi, y_lo = divmod(y % (2 * Y_HI), 2)
    return (y_lo * CORES + core) * (X * Y_HI * Z) + (x * Y_HI + y_hi) * Z + z


def body(amplitudes, singles, pair_list, mirror, slab_rows, occ_energy, vir_energy, integrals):
    owners = lax.axis_size("mem")
    groups = lax.axis_size("grp")
    member = lax.axis_index("mem").reshape(1)
    group = lax.axis_index("grp").reshape(1)
    pair_dev, _, _, width = amplitudes.shape
    half = pair_dev * owners // 2
    chunks = -(-width // LANES)
    padded = chunks * LANES

    def swap(value, flip):
        return lax.ppermute(value, "grp", [(i, i ^ flip) for i in range(groups)])

    planes = [[(x * Y_HI + y) * Z + z for x in range(X) for z in range(Z)] for y in range(Y_HI)]
    packed = pack(amplitudes, chunks)
    blocks = lax.all_to_all(packed, "mem", 0, 0, axis_index_groups=planes)
    blocks = blocks.reshape(X * Z, Y_HI, pair_dev, chunks, LANES)

    ordered = jnp.concatenate([pair_list[:half], pair_list.at[mirror[:half]].get(mode="promise_in_bounds")], axis=0)
    ints = hbm(jnp.transpose(integrals[:, :, 0, :], (1, 2, 0)))
    from_singles, high, low = early(member, ordered, singles.T, ints, padded)
    y_hi = member // Z % Y_HI
    place = jnp.concatenate([y_hi, 1 - y_hi, group])
    ours = jnp.concatenate([y_hi, y_hi])
    theirs = jnp.concatenate([y_hi, 1 - y_hi])
    blocks, from_singles, high, low, place, ours, theirs, member = lax.optimization_barrier(
        (blocks, from_singles, high, low, place, ours, theirs, member)
    )

    away = unpack(theirs, mirror, blocks)
    pairs = away.shape[1]
    from_near = lax.ppermute(away, ("grp", "mem"), [(i, neighbour(i)) for i in range(groups * owners)])
    home = unpack(ours, mirror, blocks)
    from_chip = swap(home, 2)
    from_core = swap(home, 1)
    high, low, total = own(place, home, high, low)
    passed = swap(from_near, 2)
    core_near = swap(from_near, 1)
    core_chip = swap(from_chip, 1)
    total = contract(place, 1, [from_core], 0, high, low, total)
    total = contract(place, 2, [from_chip, from_near], 0, high, low, total)
    total = contract(place, 3, [core_chip, core_near], 0, high, low, total)
    passed, total = lax.optimization_barrier((passed, total))
    core_passed = swap(passed, 1)
    total = contract(place, 0, [passed], pairs, high, low, total)
    total = contract(place, 1, [core_passed], pairs, high, low, total, from_singles)

    total, vir_energy, slab_rows = lax.optimization_barrier((total, vir_energy, slab_rows))
    parts = lax.all_to_all(total.reshape(owners, -1, LANES), "mem", 0, 0)
    energies = jnp.pad(vir_energy, (0, padded - width)).reshape(chunks, LANES).T
    virtual = virtual_sums(slab_rows.T, energies)
    return finish(member, mirror, pair_list.T, occ_energy, virtual, parts)


def solution(mesh):
    in_specs = (
        P("mem", "grp", None, None),
        P(),
        P(),
        P(),
        P("grp", None),
        P(),
        P(),
        P("grp", None, "mem", None),
    )
    out_specs = P("mem", "grp")

    return jax.shard_map(body, mesh=mesh, in_specs=in_specs, out_specs=out_specs, check_vma=False)
```
